512 devices in a mesh: gx: 32 (over z, y_lo), gy: 16 (over y_hi, x, core).
Axes of the slice: x: 4, y: 4 (y_hi: 2, y_lo: 2; y = y_hi * 2 + y_lo), z: 16, core: 2. Of those that a mesh axis runs over, the one named last changes fastest.
Arguments:
- spectrum: float32 [32, 32, 32, 32], P('gx', 'gy'), may hold values from -6 to 6
- spec_weights: float32 [4, 32, 32, 32, 32], P(None, 'gx', 'gy'), may hold values from -1 to 1
- pointwise: bfloat16 [4, 512, 256, 128], P(None, 'gx', 'gy'), may hold values from -6 to 6
- mode_counts: int32 [3], replicated, may hold values from 8 to 16, as said below
- flags: int32 [512, 256], P('gx', 'gy'), may hold values from 0 to 2
Outputs:
- field_grad: bfloat16 [4, 512, 256, 128], P(None, 'gx', 'gy')
- grad_weights: float32 [4, 32, 32, 32, 32], P(None, 'gx', 'gy')
The draws below stay inside these ranges and needn't reach their ends.
Inputs may be any that keep to these rules, and one draw needn't show every extreme that they name: `mode_counts`: entry a is the number of retained frequencies along x, y, z in turn; one entry equals 16. `flags`: 0 marks a fluid column, 1 a solid wall column, 2 an inflow column.
All inputs are finite; a program needn't handle non-finite values.
Results may differ from the reference program's by a relative error of at most 0.001.
Values sent between devices are 32-bit elements; how exact they have to be, the bound alone decides.
No kernel may reach another device: no remote copies, remote signals or barrier semaphores. Data moves between devices by JAX's collectives and lax.ppermute only.
A program may use at most 64 MiB of HBM per device.

```python
import math
import jax
import jax.numpy as jnp
from jax import lax

C = 32
M = 16
NZ = 128
K = 32
NX = 512
NY = 256


def draw_mode_counts(key, part):
    counts = jax.random.randint(jax.random.fold_in(key, 11), (3,), M // 2, M + 1)
    chosen = jax.random.randint(jax.random.fold_in(key, 12), (), 0, 3)
    return jnp.where(jnp.arange(3) == chosen, M, counts).astype(jnp.int32)


def place_ends(array, stream_key, low, high):
    shape = array.shape
    index_at = [jax.random.randint(jax.random.fold_in(stream_key, axis), (), 0, shape[axis]) for axis in range(len(shape))]
    array = array.at[tuple(index_at)].set(low)
    longest = shape.index(max(shape))
    index_at[longest] = (index_at[longest] + 1) % shape[longest]
    return array.at[tuple(index_at)].set(high)


def level_of(key, dims, shards, smallest, largest):
    def one(dim, blocks):
        steps = jax.random.uniform(jax.random.fold_in(jax.random.fold_in(key, 6), dim), (blocks,), jnp.float32, smallest / len(shards), largest / len(shards))
        return jnp.repeat(jnp.exp(steps), dims[dim] // blocks).reshape((-1,) + (1,) * (len(dims) - dim - 1))

    loudness = one(*shards[0])
    for cut in shards[1:]:
        loudness = loudness * one(*cut)
    return loudness


def gaussian(rng, extent, spread, reach, cuts=(), kind=jnp.bfloat16):
    values = spread * jax.random.normal(rng, extent, jnp.float32)
    if cuts:
        values = values * level_of(rng, extent, cuts, -0.22, 0.18)
    return jnp.clip(values, -reach, reach).astype(kind)


def setup_inputs(seed: int = 0) -> dict:
    streams_of = jax.random.split(jax.random.key(seed), 6)
    spectrum = gaussian(streams_of[0], (C, K, K, K), 1.0, 6.0, ((0, 32), (1, 16)), jnp.float32)
    spec_weights = gaussian(streams_of[1], (4, C, K, K, K), C ** -0.5, 1.0, ((1, 32), (2, 16)), jnp.float32)
    pointwise = gaussian(streams_of[2], (4, NX, NY, NZ), 1.0, 6.0, ((1, 32), (2, 16)))
    mode_counts = draw_mode_counts(jax.random.fold_in(streams_of[5], 71), 0)
    flags = place_ends(jax.random.randint(streams_of[4], (NX, NY), 0, 3), jax.random.fold_in(streams_of[4], 1), 0, 2).astype(jnp.int32)
    return dict(spectrum=spectrum, spec_weights=spec_weights, pointwise=pointwise, mode_counts=mode_counts, flags=flags)


viscosity = 0.1
penalty = 2.0
inflow_speed = 1.0
highest = lax.Precision.HIGHEST

def mode_basis(count, length, start, cells, half_modes):
    indices = jnp.arange(2 * half_modes, dtype=jnp.int32)
    freqs = jnp.where(indices < half_modes, indices, indices - half_modes + 1)
    places = start + jnp.arange(cells, dtype=jnp.int32)
    phases = freqs[:, None] * places[None, :] % length
    angles = phases.astype(jnp.float32) * jnp.float32(2.0 * math.pi / length)
    values = jnp.where(indices[:, None] < half_modes, jnp.cos(angles), jnp.sin(angles))
    keep = indices % half_modes < count
    return jnp.where(keep[:, None], values, jnp.float32(0.0)) * jnp.float32(math.sqrt(1.0 / half_modes))

def roll_diff(values, dimension):
    return (jnp.roll(values, -1, dimension) - jnp.roll(values, 1, dimension)) * 0.5

def roll_laplace(values):
    total = jnp.roll(values, -1, -3) + jnp.roll(values, 1, -3)
    total = total + jnp.roll(values, -1, -2) + jnp.roll(values, 1, -2)
    total = total + jnp.roll(values, -1, -1) + jnp.roll(values, 1, -1)
    return total - 6.0 * values

def wall_term(velocity, flags):
    solid = (flags > 0)[:, :, None]
    inflow = (flags == 2)[:, :, None]
    target = jnp.where(inflow, jnp.float32(inflow_speed), jnp.float32(0.0))
    offsets = jnp.stack([target, jnp.zeros_like(target), jnp.zeros_like(target)])
    return penalty * jnp.where(solid[None], velocity - offsets, jnp.float32(0.0))

def reference(spectrum, spec_weights, pointwise, mode_counts, flags):
    basis_x = mode_basis(mode_counts[0], NX, 0, NX, M)
    basis_y = mode_basis(mode_counts[1], NY, 0, NY, M)
    basis_z = mode_basis(mode_counts[2], NZ, 0, NZ, M)
    mixed = jnp.einsum('ocprq,cprq->oprq', spec_weights, spectrum, precision=highest)
    section = jnp.einsum('oprq,px->oxrq', mixed, basis_x, precision=highest)
    section = jnp.einsum('oxrq,ry->oxyq', section, basis_y, precision=highest)
    fields = jnp.einsum('oxyq,qz->oxyz', section, basis_z, precision=highest) + pointwise.astype(jnp.float32)
    velocity = fields[:3]
    pressure = fields[3]
    slope_x = roll_diff(velocity, -3)
    slope_y = roll_diff(velocity, -2)
    slope_z = roll_diff(velocity, -1)
    divergence = slope_x[0] + slope_y[1] + slope_z[2]
    press = jnp.stack([roll_diff(pressure, -3), roll_diff(pressure, -2), roll_diff(pressure, -1)])
    resid = velocity[0] * slope_x + velocity[1] * slope_y + velocity[2] * slope_z + press - viscosity * roll_laplace(velocity)
    back = -jnp.stack([roll_diff(divergence, -3), roll_diff(divergence, -2), roll_diff(divergence, -1)])
    back = back + jnp.stack([lax.optimization_barrier(jnp.sum(resid * slope_x, 0)), lax.optimization_barrier(jnp.sum(resid * slope_y, 0)), lax.optimization_barrier(jnp.sum(resid * slope_z, 0))])
    back = back - (roll_diff(velocity[0] * resid, -3) + roll_diff(velocity[1] * resid, -2) + roll_diff(velocity[2] * resid, -1))
    back = back - viscosity * roll_laplace(resid)
    back = back + wall_term(velocity, flags)
    back_pressure = -(roll_diff(resid[0], -3) + roll_diff(resid[1], -2) + roll_diff(resid[2], -1))
    grad_field = jnp.concatenate([back, back_pressure[None]], 0)
    section = jnp.einsum('oxyz,qz->oxyq', grad_field, basis_z, precision=highest)
    section = jnp.einsum('oxyq,ry->oxrq', section, basis_y, precision=highest)
    mixed_grad = jnp.einsum('oxrq,px->oprq', section, basis_x, precision=highest)
    scale = (2 * M) ** 1.5 / math.sqrt(NX * NY * NZ)
    grad_weights = jnp.float32(scale) * mixed_grad[:, None] * spectrum[None]
    return (grad_field.astype(jnp.bfloat16), grad_weights)
```

```python
import math

import jax
import jax.numpy as jnp
from jax import lax
from jax.sharding import PartitionSpec as P

viscosity = 0.1
penalty = 2.0
inflow_speed = 1.0
high = lax.Precision.HIGH


def mode_basis(count, length, start, cells, half_modes):
    indices = jnp.arange(2 * half_modes, dtype=jnp.int32)
    freqs = jnp.where(indices < half_modes, indices, indices - half_modes + 1)
    places = start + jnp.arange(cells, dtype=jnp.int32)
    phases = freqs[:, None] * places[None, :] % length
    angles = phases.astype(jnp.float32) * jnp.float32(2.0 * math.pi / length)
    values = jnp.where(indices[:, None] < half_modes, jnp.cos(angles), jnp.sin(angles))
    keep = indices % half_modes < count
    return jnp.where(keep[:, None], values, jnp.float32(0.0)) * jnp.float32(
        math.sqrt(1.0 / half_modes)
    )


def interior(values):
    return values[..., 1:-1, 1:-1, :]


def diff_x(values):
    return (values[..., 2:, 1:-1, :] - values[..., :-2, 1:-1, :]) * 0.5


def diff_y(values):
    return (values[..., 1:-1, 2:, :] - values[..., 1:-1, :-2, :]) * 0.5


def diff_z(values):
    middle = interior(values)
    return (jnp.roll(middle, -1, -1) - jnp.roll(middle, 1, -1)) * 0.5


def laplace(values):
    middle = interior(values)
    total = values[..., 2:, 1:-1, :] + values[..., :-2, 1:-1, :]
    total = total + values[..., 1:-1, 2:, :] + values[..., 1:-1, :-2, :]
    total = total + jnp.roll(middle, -1, -1) + jnp.roll(middle, 1, -1)
    return total - 6.0 * middle


def wall_term(velocity, flags):
    solid = (flags > 0)[:, :, None]
    inflow = (flags == 2)[:, :, None]
    target = jnp.where(inflow, jnp.float32(inflow_speed), jnp.float32(0.0))
    offsets = jnp.stack([target, jnp.zeros_like(target), jnp.zeros_like(target)])
    return penalty * jnp.where(solid[None], velocity - offsets, jnp.float32(0.0))


def residuals(padded):
    velocity = padded[:3]
    pressure = padded[3]
    slope_x = diff_x(velocity)
    slope_y = diff_y(velocity)
    slope_z = diff_z(velocity)
    inside = interior(velocity)
    divergence = slope_x[0] + slope_y[1] + slope_z[2]
    press = jnp.stack([diff_x(pressure), diff_y(pressure), diff_z(pressure)])
    resid = (
        inside[0] * slope_x
        + inside[1] * slope_y
        + inside[2] * slope_z
        + press
        - viscosity * laplace(velocity)
    )
    return (divergence, resid, (slope_x, slope_y, slope_z))


def adjoint(vel_cycle, beside_all, slopes, flags):
    div_cycle = beside_all[0]
    resid_cycle = beside_all[1:]
    resid = interior(resid_cycle)
    velocity = interior(vel_cycle)
    slope_x, slope_y, slope_z = slopes
    back = -jnp.stack([diff_x(div_cycle), diff_y(div_cycle), diff_z(div_cycle)])
    back = back + jnp.stack(
        [jnp.sum(resid * slope_x, 0), jnp.sum(resid * slope_y, 0), jnp.sum(resid * slope_z, 0)]
    )
    back = back - (
        diff_x(vel_cycle[0] * resid_cycle)
        + diff_y(vel_cycle[1] * resid_cycle)
        + diff_z(vel_cycle[2] * resid_cycle)
    )
    back = back - viscosity * laplace(resid_cycle)
    back = back + wall_term(velocity, flags)
    back_pressure = -(diff_x(resid_cycle[0]) + diff_y(resid_cycle[1]) + diff_z(resid_cycle[2]))
    return jnp.concatenate([back, back_pressure[None]], 0)


def shift_pair(head, tail, axis):
    count = lax.axis_size(axis)
    before = lax.ppermute(tail, axis, [(i, (i + 1) % count) for i in range(count)])
    after = lax.ppermute(head, axis, [((i + 1) % count, i) for i in range(count)])
    return before, after


def extended(cells, axis, dim, width):
    size = cells.shape[dim]
    head = lax.slice_in_dim(cells, 0, width, axis=dim).astype(jnp.float32)
    tail = lax.slice_in_dim(cells, size - width, size, axis=dim).astype(jnp.float32)
    before, after = shift_pair(head, tail, axis)
    return jnp.concatenate([before, cells.astype(jnp.float32), after], axis=dim)


def exchange(chunks, axis):
    return lax.all_to_all(chunks, axis, 0, 0, tiled=True)


def reduce_scattered(chunks, axis):
    return jnp.sum(exchange(chunks, axis), 0)


def gathered(part, axis):
    count = lax.axis_size(axis)
    return exchange(jnp.broadcast_to(part[None], (count,) + part.shape), axis)


def body(spectrum, spec_weights, pointwise, mode_counts, flags):
    half_modes = spectrum.shape[3] // 2
    mode_span = 2 * half_modes
    local_freqs = spectrum.shape[1]
    parts = pointwise.shape[0]
    cells_x = pointwise.shape[1]
    cells_y = pointwise.shape[2]
    cells_z = pointwise.shape[3]
    across_x = lax.axis_size("gx")
    across_y = lax.axis_size("gy")
    total_x = cells_x * across_x
    total_y = cells_y * across_y
    first_x = lax.axis_index("gx") * cells_x
    first_y = lax.axis_index("gy") * cells_y
    basis_x = mode_basis(mode_counts[0], total_x, first_x - 2, cells_x + 4, half_modes)
    basis_y = mode_basis(mode_counts[1], total_y, first_y - 2, cells_y + 4, half_modes)
    basis_z = mode_basis(mode_counts[2], cells_z, 0, cells_z, half_modes)
    wide = extended(pointwise, "gx", 1, 2)
    wide = extended(wide, "gy", 2, 2)
    partial_value = jnp.sum(spec_weights * spectrum[None], 1)
    chunks = jnp.transpose(partial_value, (1, 0, 2, 3)).reshape(across_x, -1)
    modes = gathered(reduce_scattered(chunks, "gx"), "gx")
    modes = gathered(modes.reshape(-1), "gy").reshape(mode_span, parts, mode_span, mode_span)
    section = jnp.einsum("porq,px->oxrq", modes, basis_x, precision=high)
    section = jnp.einsum("oxrq,ry->oxyq", section, basis_y, precision=high)
    fields = jnp.einsum("oxyq,qz->oxyz", section, basis_z, precision=high) + wide
    divergence, resid, slopes = residuals(fields)
    stacked = jnp.concatenate([divergence[None], resid], 0)
    vel_cycle = fields[:3, 1:-1, 1:-1]
    inner = tuple(interior(slope) for slope in slopes)
    grad_field = adjoint(vel_cycle, stacked, inner, flags)
    section = jnp.einsum("oxyz,qz->oxyq", grad_field, basis_z, precision=high)
    section = jnp.einsum("oxyq,ry->oxrq", section, basis_y[:, 2:-2], precision=high)
    projected = jnp.einsum("oxrq,px->porq", section, basis_x[:, 2:-2], precision=high)
    summed = reduce_scattered(projected.reshape(across_y, -1), "gy")
    summed = reduce_scattered(summed.reshape(across_x, -1), "gx")
    total = gathered(summed, "gx").reshape(local_freqs, parts, mode_span, mode_span)
    mixed_grad = jnp.transpose(total, (1, 0, 2, 3))
    scale = mode_span**1.5 / math.sqrt(total_x * total_y * cells_z)
    grad_weights = jnp.float32(scale) * mixed_grad[:, None] * spectrum[None]
    return (grad_field.astype(jnp.bfloat16), grad_weights)


def solution(mesh):
    return jax.shard_map(
        body,
        mesh=mesh,
        in_specs=(
            P("gx", "gy", None, None),
            P(None, "gx", "gy", None, None),
            P(None, "gx", "gy", None),
            P(),
            P("gx", "gy"),
        ),
        out_specs=(P(None, "gx", "gy", None), P(None, "gx", "gy", None, None)),
        check_vma=False,
    )
```

```python
import functools
import math

import jax
import jax.numpy as jnp
from jax import lax
from jax.experimental import pallas as pl
from jax.experimental.pallas import tpu as pltpu
from jax.sharding import PartitionSpec as P

viscosity = 0.1
penalty = 2.0
inflow_speed = 1.0
halo = 2
rim = 8


def mode_basis(count, length, places, half_modes):
    indices = jnp.arange(2 * half_modes, dtype=jnp.int32)
    freqs = jnp.where(indices < half_modes, indices, indices - half_modes + 1)
    phases = freqs[:, None] * places[None, :] % length
    angles = phases.astype(jnp.float32) * jnp.float32(2.0 * math.pi / length)
    values = jnp.where(indices[:, None] < half_modes, jnp.cos(angles), jnp.sin(angles))
    keep = indices % half_modes < count
    return jnp.where(keep[:, None], values, jnp.float32(0.0)) * jnp.float32(
        math.sqrt(1.0 / half_modes)
    )


def halves(values):
    high = values.astype(jnp.bfloat16)
    low = (values - high.astype(jnp.float32)).astype(jnp.bfloat16)
    return high, low


def stacked_rows(values):
    high, low = halves(values)
    return jnp.concatenate([high, low, high], axis=0)


def stacked_lanes(values, width):
    high, low = halves(values)
    lanes = lax.broadcasted_iota(jnp.int32, values.shape, 1)
    picked = jnp.where(lanes < 2 * width, high.astype(jnp.float32), low.astype(jnp.float32))
    return picked.astype(jnp.bfloat16)


def product(left, right, dims):
    return lax.dot_general(
        left, right, (dims, ((), ())), preferred_element_type=jnp.float32
    )


def rolled(values, shift, axis):
    return pltpu.roll(values, shift % values.shape[axis], axis)


def mix_kernel(weights_ref, spectrum_ref, out_ref):
    parts, channels, freqs = weights_ref.shape[:3]
    rows = weights_ref.shape[3]
    for freq in range(freqs):
        pieces = []
        for part in range(parts):
            total = weights_ref[part, 0, freq] * spectrum_ref[0, freq]
            for channel in range(1, channels):
                total = total + weights_ref[part, channel, freq] * spectrum_ref[channel, freq]
            pieces.append(total)
        out_ref[freq * rows : (freq + 1) * rows, :] = jnp.concatenate(pieces, axis=1)


def spread_kernel(scale, total_ref, spectrum_ref, out_ref):
    parts, channels, freqs, rows, cols = out_ref.shape
    for freq in range(freqs):
        for part in range(parts):
            piece = total_ref[freq * rows : (freq + 1) * rows, part * cols : (part + 1) * cols]
            for channel in range(channels):
                out_ref[part, channel, freq] = scale * piece * spectrum_ref[channel, freq]


def middle_kernel(
    modes_ref,
    basis_x_ref,
    lift_y_ref,
    drop_y_ref,
    blocks_ref,
    point_ref,
    before_ref,
    after_ref,
    edges_ref,
    flags_ref,
    grad_ref,
    out_ref,
    along_ref,
    field_ref,
    resid_ref,
    slope_ref,
    back_ref,
    drop_ref,
):
    parts, cells_x, cells_y, cells_z = point_ref.shape
    freqs, wide_x = basis_x_ref.shape
    rows = modes_ref.shape[0] // freqs
    tall = cells_y + rim
    group = 4
    lift_y = stacked_lanes(lift_y_ref[...], rows)
    drop_y = stacked_lanes(drop_y_ref[...], cells_y)
    block_high, block_low = halves(blocks_ref[...])

    def spread_x(pair, carry):
        first = pair * 2
        left = jnp.zeros((rows, modes_ref.shape[1]), jnp.float32)
        right = left
        for freq in range(freqs):
            value = modes_ref[freq * rows : (freq + 1) * rows, :]
            left = left + basis_x_ref[freq, first] * value
            right = right + basis_x_ref[freq, first + 1] * value
        along_ref[first] = left
        along_ref[first + 1] = right
        return carry

    lax.fori_loop(0, wide_x // 2, spread_x, 0)

    for start in range(0, wide_x, group):
        joined = jnp.concatenate([along_ref[start + k] for k in range(group)], axis=1)
        lifted = product(lift_y, stacked_rows(joined), ((1,), (0,)))
        width = modes_ref.shape[1]
        sheet = jnp.concatenate(
            [lifted[:, k * width : (k + 1) * width] for k in range(group)], axis=0
        )
        high, low = halves(sheet)
        full = product(high, block_high, ((1,), (0,)))
        full = full + product(low, block_high, ((1,), (0,)))
        full = full + product(high, block_low, ((1,), (0,)))
        for k in range(group):
            slab = start + k
            for part in range(parts):
                tile = full[k * tall : (k + 1) * tall, part * cells_z : (part + 1) * cells_z]
                if slab < halo:
                    inner = before_ref[part, slab]
                elif slab >= halo + cells_x:
                    inner = after_ref[part, slab - halo - cells_x]
                else:
                    inner = point_ref[part, slab - halo].astype(jnp.float32)
                field_ref[part, slab, :rim] = tile[:rim] + edges_ref[part, slab]
                field_ref[part, slab, rim:] = tile[rim:] + inner

    def beside(values):
        return (
            rolled(values, -1, 0),
            rolled(values, 1, 0),
            rolled(values, -1, 1),
            rolled(values, 1, 1),
        )

    def residuals(slab, carry):
        here = [field_ref[part, slab] for part in range(4)]
        slopes = []
        spreads = []
        for part in range(4):
            ahead = field_ref[part, slab + 1]
            behind = field_ref[part, slab - 1]
            up, down, right, left = beside(here[part])
            slopes.append(((ahead - behind) * 0.5, (up - down) * 0.5, (right - left) * 0.5))
            if part < 3:
                total = ((ahead + behind) + (up + down)) + (right + left)
                spreads.append(total - 6.0 * here[part])
        for i in range(3):
            value = here[0] * slopes[i][0] + here[1] * slopes[i][1] + here[2] * slopes[i][2]
            resid_ref[i, slab - 1] = value + slopes[3][i] - viscosity * spreads[i]
            for k in range(3):
                slope_ref[3 * k + i, slab - 1] = slopes[i][k][rim:]
        resid_ref[3, slab - 1] = slopes[0][0] + slopes[1][1] + slopes[2][2]
        return carry

    lax.fori_loop(1, wide_x - 1, residuals, 0)

    def adjoints(cell, carry):
        middle = cell + 1
        slab = cell + halo
        here = [resid_ref[i, middle] for i in range(3)]
        ahead = [resid_ref[i, middle + 1, rim:] for i in range(3)]
        behind = [resid_ref[i, middle - 1, rim:] for i in range(3)]
        core = [value[rim:] for value in here]
        drift_y = field_ref[1, slab]
        drift_z = field_ref[2, slab, rim:]
        drift_ahead = field_ref[0, slab + 1, rim:]
        drift_behind = field_ref[0, slab - 1, rim:]
        flag = flags_ref[cell]
        solid = flag > 0
        target = jnp.where(flag == 2, jnp.float32(inflow_speed), jnp.float32(0.0))
        source = resid_ref[3, middle]
        up, down = rolled(source, -1, 0)[rim:], rolled(source, 1, 0)[rim:]
        source_core = source[rim:]
        right, left = rolled(source_core, -1, 1), rolled(source_core, 1, 1)
        pull = [
            (resid_ref[3, middle + 1, rim:] - resid_ref[3, middle - 1, rim:]) * 0.5,
            (up - down) * 0.5,
            (right - left) * 0.5,
        ]
        press = []
        backs = []
        for k in range(3):
            up, down = rolled(here[k], -1, 0)[rim:], rolled(here[k], 1, 0)[rim:]
            right, left = rolled(core[k], -1, 1), rolled(core[k], 1, 1)
            press.append(((ahead[k] - behind[k]), (up - down), (right - left))[k] * 0.5)
            spread = ((ahead[k] + behind[k]) + (up + down)) + (right + left) - 6.0 * core[k]
            flux_y = drift_y * here[k]
            flux_z = drift_z * core[k]
            flux = drift_ahead * ahead[k] - drift_behind * behind[k]
            flux = flux + (rolled(flux_y, -1, 0)[rim:] - rolled(flux_y, 1, 0)[rim:])
            flux = flux + (rolled(flux_z, -1, 1) - rolled(flux_z, 1, 1))
            value = core[0] * slope_ref[3 * k, middle]
            value = value + core[1] * slope_ref[3 * k + 1, middle]
            value = value + core[2] * slope_ref[3 * k + 2, middle]
            value = value - pull[k] - 0.5 * flux - viscosity * spread
            velocity = field_ref[k, slab, rim:]
            offset = velocity - target if k == 0 else velocity
            value = value + penalty * jnp.where(solid, offset, jnp.float32(0.0))
            backs.append(value)
        backs.append(-((press[0] + press[1]) + press[2]))
        spot = pl.ds(pl.multiple_of(cell * cells_y, cells_y), cells_y)
        for part in range(4):
            grad_ref[part, cell] = backs[part].astype(grad_ref.dtype)
            back_ref[spot, part * cells_z : (part + 1) * cells_z] = backs[part]
        return carry

    lax.fori_loop(0, cells_x, adjoints, 0)

    high, low = halves(back_ref[...])
    flat = product(high, block_high, ((1,), (1,)))
    flat = flat + product(low, block_high, ((1,), (1,)))
    flat = flat + product(high, block_low, ((1,), (1,)))
    for start in range(0, cells_x, group):
        joined = jnp.concatenate(
            [flat[(start + k) * cells_y : (start + k + 1) * cells_y] for k in range(group)],
            axis=1,
        )
        dropped = product(drop_y, stacked_rows(joined), ((1,), (0,)))
        width = flat.shape[1]
        for k in range(group):
            drop_ref[start + k] = dropped[:, k * width : (k + 1) * width]

    def collect_x(pair, carry):
        first = pair * 2
        left = jnp.zeros((rows, modes_ref.shape[1]), jnp.float32)
        right = left
        for cell in range(cells_x):
            value = drop_ref[cell]
            left = left + basis_x_ref[first, cell + halo] * value
            right = right + basis_x_ref[first + 1, cell + halo] * value
        spot = pl.ds(pl.multiple_of(first * rows, rows), rows)
        out_ref[spot, :] = left
        spot = pl.ds(pl.multiple_of((first + 1) * rows, rows), rows)
        out_ref[spot, :] = right
        return carry

    lax.fori_loop(0, freqs // 2, collect_x, 0)


def middle(modes, basis_x, lift_y, drop_y, blocks, point, before, after, edges, flags):
    parts, cells_x, cells_y, cells_z = point.shape
    rows = drop_y.shape[0]
    lanes = modes.shape[1]
    wide_x = cells_x + 2 * halo
    tall = cells_y + rim
    vmem = pl.BlockSpec(memory_space=pltpu.VMEM)
    smem = pl.BlockSpec(memory_space=pltpu.SMEM)
    return pl.pallas_call(
        middle_kernel,
        name="middle",
        in_specs=[vmem, smem] + [vmem] * 8,
        out_specs=[vmem, vmem],
        out_shape=[
            jax.ShapeDtypeStruct(point.shape, jnp.bfloat16),
            jax.ShapeDtypeStruct(modes.shape, jnp.float32),
        ],
        scratch_shapes=[
            pltpu.VMEM((wide_x, rows, lanes), jnp.float32),
            pltpu.VMEM((parts, wide_x, tall, cells_z), jnp.float32),
            pltpu.VMEM((4, cells_x + 2, tall, cells_z), jnp.float32),
            pltpu.VMEM((9, cells_x + 2, cells_y, cells_z), jnp.float32),
            pltpu.VMEM((cells_x * cells_y, parts * cells_z), jnp.float32),
            pltpu.VMEM((cells_x, rows, lanes), jnp.float32),
        ],
    )(modes, basis_x, lift_y, drop_y, blocks, point, before, after, edges, flags)


def shift_pair(head, tail, axis):
    count = lax.axis_size(axis)
    before = lax.ppermute(tail, axis, [(i, (i + 1) % count) for i in range(count)])
    after = lax.ppermute(head, axis, [((i + 1) % count, i) for i in range(count)])
    return before, after


def exchange(chunks, axis):
    return lax.all_to_all(chunks, axis, 0, 0, tiled=True)


def reduce_scattered(chunks, axis):
    count = lax.axis_size(axis)
    pieces = exchange(chunks, axis)
    return jnp.sum(pieces.reshape((count, -1) + chunks.shape[1:]), 0)


def gathered(part, axis):
    count = lax.axis_size(axis)
    copies = jnp.broadcast_to(part[None], (count,) + part.shape)
    return exchange(copies.reshape((-1,) + part.shape[1:]), axis)


def body(spectrum, spec_weights, pointwise, mode_counts, flags):
    half_modes = spectrum.shape[3] // 2
    mode_span = 2 * half_modes
    local_freqs = spectrum.shape[1]
    parts, cells_x, cells_y, cells_z = pointwise.shape
    total_x = cells_x * lax.axis_size("gx")
    total_y = cells_y * lax.axis_size("gy")
    first_x = lax.axis_index("gx") * cells_x
    first_y = lax.axis_index("gy") * cells_y
    lanes = parts * mode_span
    vmem = pl.BlockSpec(memory_space=pltpu.VMEM)

    with jax.named_scope("mix"):
        chunks = pl.pallas_call(
            mix_kernel,
            name="mix",
            in_specs=[vmem, vmem],
            out_specs=vmem,
            out_shape=jax.ShapeDtypeStruct((local_freqs * mode_span, lanes), jnp.float32),
        )(spec_weights, spectrum)
    with jax.named_scope("sum_modes"):
        part = reduce_scattered(chunks, "gx")

    with jax.named_scope("halo_x"):
        head = pointwise[:, :halo].astype(jnp.float32)
        tail = pointwise[:, cells_x - halo :].astype(jnp.float32)
        before, after = shift_pair(head, tail, "gx")
    with jax.named_scope("halo_y"):
        sides = []
        for low in (0, cells_y - halo):
            own = pointwise[:, :, low : low + halo].astype(jnp.float32)
            ends = [before[:, :, low : low + halo], after[:, :, low : low + halo]]
            sides.append(jnp.concatenate([ends[0], own, ends[1]], 1))
        under, over = shift_pair(sides[0], sides[1], "gy")
        gap = jnp.zeros((parts, cells_x + 2 * halo, rim - 2 * halo, cells_z), jnp.float32)
        edges = jnp.concatenate([over, gap, under], 2)

    places_x = first_x - halo + jnp.arange(cells_x + 2 * halo, dtype=jnp.int32)
    rows_y = jnp.arange(cells_y + rim, dtype=jnp.int32)
    places_y = first_y + jnp.where(rows_y < halo, cells_y + rows_y, rows_y - rim)
    basis_x = mode_basis(mode_counts[0], total_x, places_x, half_modes)
    basis_y = mode_basis(mode_counts[1], total_y, places_y, half_modes)
    basis_z = mode_basis(
        mode_counts[2], cells_z, jnp.arange(cells_z, dtype=jnp.int32), half_modes
    )
    lift_y = jnp.tile(basis_y.T, (1, 3))
    drop_y = jnp.tile(basis_y[:, rim:], (1, 3))
    same = jnp.arange(lanes)[:, None] // mode_span == jnp.arange(parts * cells_z)[None] // cells_z
    blocks = jnp.where(same, jnp.tile(basis_z, (parts, parts)), jnp.float32(0.0))
    columns = jnp.broadcast_to(flags[:, :, None], flags.shape + (cells_z,))

    with jax.named_scope("share_modes"):
        modes = gathered(part, "gx")
    with jax.named_scope("share_freqs"):
        modes = gathered(modes, "gy")
    with jax.named_scope("middle"):
        grad_field, projected = middle(
            modes, basis_x, lift_y, drop_y, blocks, pointwise, before, after, edges, columns
        )
    with jax.named_scope("sum_y"):
        summed = reduce_scattered(projected, "gy")
    with jax.named_scope("sum_x"):
        summed = reduce_scattered(summed, "gx")
    with jax.named_scope("share_sums"):
        total = gathered(summed, "gx")
    scale = mode_span**1.5 / math.sqrt(total_x * total_y * cells_z)
    with jax.named_scope("spread"):
        grad_weights = pl.pallas_call(
            functools.partial(spread_kernel, scale),
            name="spread",
            in_specs=[vmem, vmem],
            out_specs=vmem,
            out_shape=jax.ShapeDtypeStruct(spec_weights.shape, jnp.float32),
        )(total, spectrum)
    return (grad_field, grad_weights)


def solution(mesh):
    return jax.shard_map(
        body,
        mesh=mesh,
        in_specs=(
            P("gx", "gy", None, None),
            P(None, "gx", "gy", None, None),
            P(None, "gx", "gy", None),
            P(),
            P("gx", "gy"),
        ),
        out_specs=(P(None, "gx", "gy", None), P(None, "gx", "gy", None, None)),
        check_vma=False,
    )
```
